32 devices in a mesh: facet: 8 (over y, x, core), sub: 4 (over z).
Axes of the slice: x: 2, y: 2, z: 4, core: 2. Of those that a mesh axis runs over, the one named last changes fastest.
Arguments:
- facet_spec: bfloat16 [8, 2, 704, 448], P('facet'), may hold values from -3 to 3
- worker_of_subgrid: int32 [32], replicated, may hold values from 0 to 31, each once
- vis_count: int32 [32], P(('facet', 'sub')), may hold values from 512 to 8192, as said below
- bin_offsets: int32 [32, 2, 8192], P(('facet', 'sub')), may hold values from 0 to 248
- bin_fractions: float32 [32, 2, 8192], P(('facet', 'sub')), may hold values from 0 to 1
- observed: float32 [32, 2, 8192], P(('facet', 'sub')), may hold values from -6 to 6
Outputs:
- residual_vis: float32 [32, 2, 8192], P(('facet', 'sub'))
- facet_update: float32 [8, 2, 704, 448], P('facet', None, 'sub')
The draws below stay inside these ranges and needn't reach their ends.
Inputs may be any that keep to these rules, and one draw needn't show every extreme that they name: `worker_of_subgrid`: a permutation of the subgrids. `vis_count`: some device row has all 8192 slots live in every draw.
All inputs are finite; a program needn't handle non-finite values.
Results may differ from the reference program's by a relative error of at most 0.014.
Values may be sent and summed in bfloat16 or wider, within the bound.
A program may use at most 128 MiB of HBM per device.

```python
import math
import jax
import jax.numpy as jnp
from jax import lax

SUB = 256
MC = 256
STEP = 64
KS = 8
VMAX = 8192
POS_V = 4
FACETS = 8
SUBGRIDS = 32
PR = 704
PC = 448


def draw_vis_count(key, part):
    low_key = jax.random.fold_in(key, 11)
    crowd_key = jax.random.fold_in(key, 12)
    pick_key = jax.random.fold_in(key, 13)
    base = jax.random.randint(low_key, (SUBGRIDS,), VMAX // 16, VMAX // 2 + 1)
    crowded = jax.random.randint(crowd_key, (SUBGRIDS,), 0, 8) == 0
    chosen = jax.random.randint(pick_key, (), 0, SUBGRIDS)
    crowded = crowded | (jnp.arange(SUBGRIDS) == chosen)
    return jnp.where(crowded, VMAX, base).astype(jnp.int32)


def set_ends(entries, own_key, least, largest):
    spot = [jax.random.randint(jax.random.fold_in(own_key, axis), (), 0, length) for axis, length in enumerate(entries.shape)]
    main_axis = entries.shape.index(max(entries.shape))
    next_to = spot[:main_axis] + [(spot[main_axis] + 1) % entries.shape[main_axis]] + spot[main_axis + 1:]
    return entries.at[tuple(spot)].set(least).at[tuple(next_to)].set(largest)


def shard_levels(key, dims, split, smallest, largest):
    def one(dim, parts):
        heights = jax.random.uniform(jax.random.fold_in(jax.random.fold_in(key, 6), dim), (parts,), jnp.float32, smallest / len(split), largest / len(split))
        return jnp.repeat(jnp.exp(heights), dims[dim] // parts).reshape((-1,) + (1,) * (len(dims) - dim - 1))

    gain = one(*split[0])
    for cut in split[1:]:
        gain = gain * one(*cut)
    return gain


def scatter_about(key, extent, spread, most, pieces=(), kind=jnp.bfloat16):
    values = spread * jax.random.normal(key, extent, jnp.float32)
    if pieces:
        values = values * shard_levels(key, extent, pieces, -0.22, 0.18)
    return jnp.clip(values, -most, most).astype(kind)


def setup_inputs(seed: int = 0) -> dict:
    arg_keys = jax.random.split(jax.random.key(seed), 7)
    facet_spec = scatter_about(arg_keys[0], (FACETS, 2, PR, PC), 0.5, 3.0, ((0, 8),))
    worker_of_subgrid = jax.random.permutation(arg_keys[1], SUBGRIDS).astype(jnp.int32)
    vis_count = draw_vis_count(jax.random.fold_in(arg_keys[6], 71), 0)
    bin_offsets = set_ends(jax.random.randint(arg_keys[3], (SUBGRIDS, 2, VMAX), 0, SUB - KS + 1), jax.random.fold_in(arg_keys[3], 1), 0, SUB - KS).astype(jnp.int32)
    bin_fractions = jnp.clip(1.0 * jax.random.uniform(arg_keys[4], (SUBGRIDS, 2, VMAX), jnp.float32) ** shard_levels(arg_keys[4], (SUBGRIDS, 2, VMAX), ((0, 32),), -0.2, 0.2), 0.0, 1.0)
    observed = scatter_about(arg_keys[5], (SUBGRIDS, 2, VMAX), 1.0, 6.0, ((0, 32),), jnp.float32)
    return dict(facet_spec=facet_spec, worker_of_subgrid=worker_of_subgrid, vis_count=vis_count, bin_offsets=bin_offsets, bin_fractions=bin_fractions, observed=observed)


TWO_PI = 2.0 * math.pi


def phase_table(offset, facets, swapped, conj_sign):
    sub_index = jnp.arange(SUB, dtype=jnp.int32) - SUB // 2
    win_index = jnp.arange(MC, dtype=jnp.int32) - MC // 2
    if swapped:
        sub_part = sub_index[None, :]
        win_part = win_index[:, None]
    else:
        sub_part = sub_index[:, None]
        win_part = win_index[None, :]
    modulus = SUB * facets
    residue = jnp.mod(sub_part * win_part * facets + sub_part * offset, modulus)
    angles = residue.astype(jnp.float32) * (TWO_PI / modulus)
    factor = MC ** -0.5
    return jnp.stack([jnp.cos(angles) * factor, conj_sign * jnp.sin(angles) * factor]).astype(jnp.bfloat16)


def wide_dot(first_part, second_part):
    return jnp.dot(first_part.astype(jnp.float32), second_part.astype(jnp.float32), precision=lax.Precision.HIGHEST, preferred_element_type=jnp.float32)


def pair_dot(first_pair, second_pair):
    real_real = wide_dot(first_pair[0], second_pair[0])
    imag_imag = wide_dot(first_pair[1], second_pair[1])
    real_imag = wide_dot(first_pair[0], second_pair[1])
    imag_real = wide_dot(first_pair[1], second_pair[0])
    return jnp.stack([real_real - imag_imag, real_imag + imag_real])


def kernel_rows(offsets, fractions):
    cells = jnp.arange(SUB, dtype=jnp.int32)[None, :] - offsets[:, None]
    distance = cells.astype(jnp.float32) - fractions[:, None] - (0.5 * KS - 1.0)
    inside = (cells >= 0) & (cells < KS)
    weights = jnp.where(inside, 0.5 * jnp.exp(-jnp.square(distance * (9.0 / KS))), 0.0)
    return weights.astype(jnp.bfloat16)


def subgrid_holder(worker):
    total_rows = worker.shape[0]
    slot_ids = jnp.arange(total_rows, dtype=jnp.int32)
    matches = (worker[None, :] == slot_ids[:, None]).astype(jnp.int32)
    return jnp.sum(matches * slot_ids[None, :], axis=1).astype(jnp.int32)


def adjoint_window(resid_grid, facet_id, facets):
    left_table = phase_table(facet_id, facets, True, -1.0)
    right_table = phase_table(jnp.mod(5 * facet_id + 3, facets), facets, False, -1.0)
    partial_value = pair_dot(left_table, resid_grid).astype(jnp.bfloat16)
    return pair_dot(partial_value, right_table).astype(jnp.bfloat16)


def reference(facet_spec, worker_of_subgrid, vis_count, bin_offsets, bin_fractions, observed):
    facets = facet_spec.shape[0]
    holder = subgrid_holder(worker_of_subgrid)
    facet_ids = jnp.arange(facets, dtype=jnp.int32)
    anchor = jnp.int32(0)

    def device_row(planes, device_id):
        subgrid = holder[device_id]
        top_row = ((subgrid // POS_V) * STEP).astype(jnp.int32)
        left_col = ((subgrid % POS_V) * STEP).astype(jnp.int32)

        def add_facet(running, facet_id):
            contribution = lax.dynamic_slice(facet_spec, (facet_id, anchor, top_row, left_col), (1, 2, MC, MC))[0]
            left_table = phase_table(facet_id, facets, False, 1.0)
            right_table = phase_table(jnp.mod(5 * facet_id + 3, facets), facets, True, 1.0)
            partial_value = pair_dot(left_table, contribution).astype(jnp.bfloat16)
            return running + pair_dot(partial_value, right_table), None

        grid_sum, _ = lax.scan(add_facet, jnp.zeros((2, SUB, SUB), jnp.float32), facet_ids)
        grid_half = grid_sum.astype(jnp.bfloat16)
        grid_cat = jnp.concatenate([grid_half[0], grid_half[1]], axis=1)
        offsets = bin_offsets[device_id]
        fractions = bin_fractions[device_id]
        observed_rows = observed[device_id]
        u_weights = kernel_rows(offsets[0], fractions[0])
        v_weights = kernel_rows(offsets[1], fractions[1])
        product = wide_dot(u_weights, grid_cat)
        v_float = v_weights.astype(jnp.float32)
        model_real = jnp.sum(product[:, :SUB] * v_float, axis=1)
        model_imag = jnp.sum(product[:, SUB:] * v_float, axis=1)
        live_mask = jnp.arange(VMAX, dtype=jnp.int32) < vis_count[device_id]
        real_part = jnp.where(live_mask, observed_rows[0] - model_real, 0.0)
        imag_part = jnp.where(live_mask, observed_rows[1] - model_imag, 0.0)
        weighted = jnp.concatenate([real_part[:, None] * v_float, imag_part[:, None] * v_float], axis=1).astype(jnp.bfloat16)
        gridded = lax.dot_general(u_weights.astype(jnp.float32), weighted.astype(jnp.float32), (((0,), (0,)), ((), ())), precision=lax.Precision.HIGHEST, preferred_element_type=jnp.float32)
        resid_grid = jnp.stack([gridded[:, :SUB], gridded[:, SUB:]]).astype(jnp.bfloat16)

        def one_window(facet_id):
            return adjoint_window(resid_grid, facet_id, facets)

        windows = lax.map(one_window, facet_ids)
        current = lax.dynamic_slice(planes, (anchor, anchor, top_row, left_col), (facets, 2, MC, MC))
        planes = lax.dynamic_update_slice(planes, current + windows.astype(jnp.float32), (anchor, anchor, top_row, left_col))
        return planes, jnp.stack([real_part, imag_part])

    planes, residual = lax.scan(device_row, jnp.zeros((facets, 2, PR, PC), jnp.float32), jnp.arange(SUBGRIDS, dtype=jnp.int32))
    return residual, planes
```

```python
import functools
import math

import jax
import jax.numpy as jnp
import numpy as np
from jax import lax
from jax.experimental import pallas as pl
from jax.experimental.pallas import tpu as pltpu
from jax.sharding import PartitionSpec as P

SUB = 256
MC = 256
STEP = 64
KS = 8
VB = 512
MESH = pl.DeviceIdType.MESH
VMEM = pl.BlockSpec(memory_space=pltpu.VMEM)
SMEM = pl.BlockSpec(memory_space=pltpu.SMEM)
F32 = jnp.float32
BF16 = jnp.bfloat16


def flip(index, bit):
    return index + bit - 2 * bit * ((index // bit) % 2)


def bits_of(count):
    return [1 << level for level in range(count.bit_length() - 1)]


def routes(count):
    bits = bits_of(count)
    return (bits, bits[:1] + bits[:0:-1])


def greet(count):
    me = lax.axis_index("facet")
    barrier = pltpu.get_barrier_semaphore()
    bits = bits_of(count)
    for bit in bits:
        pl.semaphore_signal(
            barrier, inc=1, device_id={"facet": flip(me, bit)}, device_id_type=MESH
        )
    pl.semaphore_wait(barrier, len(bits))


def remote(src, dst, send, recv, axis, target):
    return pltpu.make_async_remote_copy(
        src_ref=src,
        dst_ref=dst,
        send_sem=send,
        recv_sem=recv,
        device_id={axis: target},
        device_id_type=MESH,
    )


def transform_kernel(facets, targets, spec, left_table, right_table, slabs):
    cols = spec.shape[3]

    def transform(slab, carry):
        top = pl.multiple_of(targets[0, slab], STEP)
        left = pl.multiple_of(targets[1, slab], STEP)
        window = jnp.concatenate(
            [spec[0, 0, pl.ds(top, MC), :], spec[0, 1, pl.ds(top, MC), :]], axis=0
        )
        table = right_table[pl.ds(left, cols), :]
        mixed = jnp.dot(window, table, preferred_element_type=F32)
        real = mixed[:MC, :SUB] - mixed[MC:, SUB:]
        imag = mixed[:MC, SUB:] + mixed[MC:, :SUB]
        half = jnp.concatenate([real, imag], axis=0).astype(BF16)
        value = jnp.dot(left_table[...], half, preferred_element_type=F32)
        slabs[slab] = value.astype(BF16).reshape(2, SUB, SUB)
        return carry

    lax.fori_loop(0, facets, transform, 0)


def halve_kernel(facets, slabs, grid_out, total, landed, send, recv):
    me = lax.axis_index("facet")
    greet(facets)
    orders = routes(facets)
    held = [list(range(facets))] * 2
    sent = []
    for level in range(len(orders[0])):
        last = level == len(orders[0]) - 1
        arriving = []
        for part in range(2):
            bit = orders[part][level]
            for slab in reversed([s for s in held[part] if s & bit]):
                source = slabs if level == 0 else total
                copy = remote(
                    source.at[slab, part], landed.at[level, slab - bit, part],
                    send.at[2 * level + part, slab], recv.at[2 * level + part, slab - bit],
                    "facet", flip(me, bit),
                )
                copy.start()
                sent.append(copy)
                arriving.append((copy, slab - bit, part))
            held[part] = [s for s in held[part] if not s & bit]
        for copy, slab, part in arriving:
            copy.wait_recv()
            source = slabs if level == 0 else total
            value = source[slab, part].astype(F32) + landed[level, slab, part].astype(F32)
            if last:
                grid_out[part] = value.astype(BF16)
            else:
                total[slab, part] = value.astype(BF16)
    for copy in sent:
        copy.wait_send()


def kernel_columns(offsets, fractions):
    cells = lax.broadcasted_iota(jnp.int32, (SUB, offsets.shape[1]), 0).astype(F32)
    scale = math.sqrt(math.log2(math.e)) * 9.0 / KS
    centred = cells - (offsets.astype(F32) + (0.5 * KS - 0.5))
    distance = centred * scale - (fractions - 0.5) * scale
    inside = jnp.abs(centred) < 0.5 * KS
    return jnp.where(inside, jnp.exp2(-1.0 - distance * distance), 0.0).astype(BF16)


def vis_kernel(count, grid, offsets, fractions, observed, residual, gridded, flipped, total):
    slots = offsets.shape[2]
    live_count = count[0]
    flipped[:SUB] = grid[0].astype(F32).T.astype(BF16)
    flipped[SUB:] = grid[1].astype(F32).T.astype(BF16)
    total[...] = jnp.zeros_like(total)
    residual[...] = jnp.zeros_like(residual)

    def block(index, carry):
        first = pl.multiple_of(index * VB, VB)
        span = pl.ds(first, VB)
        u_weights = kernel_columns(offsets[0, 0:1, span], fractions[0, 0:1, span])
        v_weights = kernel_columns(offsets[0, 1:2, span], fractions[0, 1:2, span])
        v_float = v_weights.astype(F32)
        product = jnp.dot(flipped[...], u_weights, preferred_element_type=F32)
        live = first + lax.broadcasted_iota(jnp.int32, (1, VB), 1) < live_count
        weighted = []
        for part in range(2):
            model = jnp.sum(product[part * SUB : (part + 1) * SUB] * v_float, axis=0, keepdims=True)
            row = jnp.where(live, observed[0, part : part + 1, span] - model, 0.0)
            residual[0, part : part + 1, span] = row
            weighted.append((row * v_float).astype(BF16))
        total[...] += lax.dot_general(
            u_weights,
            jnp.concatenate(weighted, axis=0),
            (((1,), (1,)), ((), ())),
            preferred_element_type=F32,
        )
        return carry

    lax.fori_loop(0, (live_count + VB - 1) // VB, block, 0)
    gridded[0] = total[:, :SUB].astype(BF16)
    gridded[1] = total[:, SUB:].astype(BF16)


def gather_kernel(facets, own, everyone, slabs, send, recv):
    me = lax.axis_index("facet")
    greet(facets)
    slabs[0] = own[...]
    orders = [order[:0:-1] + order[:1] for order in routes(facets)]
    held = [[0], [0]]
    sent = []
    for level in range(len(orders[0])):
        arriving = []
        for part in range(2):
            bit = orders[part][level]
            for slab in held[part]:
                copy = remote(
                    slabs.at[slab, part], slabs.at[slab + bit, part],
                    send.at[part, slab + bit], recv.at[part, slab + bit],
                    "facet", flip(me, bit),
                )
                copy.start()
                arriving.append(copy)
            held[part] = held[part] + [s + bit for s in held[part]]
        for copy in arriving:
            copy.wait_recv()
        sent += arriving
    everyone[...] = slabs[...]
    for copy in sent:
        copy.wait_send()


def adjoint_kernel(facets, targets, everyone, left_table, right_table, pieces, plane):
    cols = plane.shape[2]
    chunk = pieces.shape[2]
    plane[...] = jnp.zeros_like(plane)

    def add_source(slab, carry):
        top = pl.multiple_of(targets[0, slab], STEP)
        left = pl.multiple_of(targets[1, slab], STEP)
        source = everyone[slab].reshape(2 * SUB, SUB)
        half = jnp.dot(left_table[...], source, preferred_element_type=F32)
        real = half[:MC]
        imag = half[MC:]
        stacked = jnp.concatenate(
            [jnp.concatenate([real, imag], axis=1), jnp.concatenate([imag, -real], axis=1)], axis=0
        ).astype(BF16)
        table = right_table[pl.ds(left, cols), :]
        window = lax.dot_general(
            stacked, table, (((1,), (1,)), ((), ())), preferred_element_type=F32
        )
        plane[0, pl.ds(top, MC), :] += window[:MC]
        plane[1, pl.ds(top, MC), :] += window[MC:]
        return carry

    lax.fori_loop(0, facets, add_source, 0)
    for piece in range(pieces.shape[0]):
        pieces[piece] = plane[:, piece * chunk : (piece + 1) * chunk, :].astype(BF16)


def spread_kernel(groups, pieces, update, landed, send, recv):
    me = lax.axis_index("sub")
    barrier = pltpu.get_barrier_semaphore()
    for hop in range(1, groups):
        pl.semaphore_signal(
            barrier, inc=1, device_id={"sub": (me + hop) % groups}, device_id_type=MESH
        )
    pl.semaphore_wait(barrier, groups - 1)
    copies = []
    for hop in range(1, groups):
        to = (me + hop) % groups
        copy = remote(
            pieces.at[to], landed.at[hop - 1], send.at[hop - 1], recv.at[hop - 1], "sub", to
        )
        copy.start()
        copies.append(copy)
    value = pieces[me].astype(F32)
    for hop, copy in enumerate(copies):
        copy.wait_recv()
        value = value + landed[hop].astype(F32)
    update[0] = value
    for copy in copies:
        copy.wait_send()


def phases(facets):
    modulus = SUB * facets
    centred = np.arange(SUB) - SUB // 2
    base = np.exp(2j * np.pi * (np.outer(centred, centred) * facets % modulus) / modulus)
    turn = np.exp(2j * np.pi * (np.outer(np.arange(facets), centred) % modulus) / modulus)
    pair = lambda z: jnp.asarray(np.stack([z.real, z.imag]).astype(np.float32))
    return pair(base * MC ** (-0.5)), pair(turn)


def turned(base, turn):
    return (base[0] * turn[0] - base[1] * turn[1], base[0] * turn[1] + base[1] * turn[0])


def on_device(facet_spec, worker_of_subgrid, vis_count, bin_offsets, bin_fractions, observed):
    facets = lax.axis_size("facet")
    pos_v = lax.axis_size("sub")
    me = lax.axis_index("facet")
    sub_rank = lax.axis_index("sub")
    rows = facet_spec.shape[2]
    cols = facet_spec.shape[3]
    pad = (pos_v - 1) * STEP
    slots = bin_offsets.shape[2]

    wanted = jnp.bitwise_xor(jnp.arange(facets, dtype=jnp.int32), me) * pos_v + sub_rank
    ids = jnp.arange(worker_of_subgrid.shape[0], dtype=jnp.int32)
    targets = jnp.sum(
        jnp.where(worker_of_subgrid[None, :] == wanted[:, None], ids[None, :], 0), axis=1
    ).astype(jnp.int32)
    targets = jnp.stack([targets // pos_v * STEP, pad - targets % pos_v * STEP])

    base, turn = phases(facets)
    turn_u = lax.dynamic_index_in_dim(turn, me, 1, keepdims=False)
    turn_v = lax.dynamic_index_in_dim(turn, (5 * me + 3) % facets, 1, keepdims=False)
    qa = turned(base, turn_u[:, :, None])
    qa_t = turned(base, turn_u[:, None, :])
    qb_t = turned(base, turn_v[:, None, :])
    join = lambda a, b, c, d: jnp.concatenate(
        [jnp.concatenate([a, b], 1), jnp.concatenate([c, d], 1)], 0
    ).astype(BF16)
    left = join(qa[0], -qa[1], qa[1], qa[0])
    left_adjoint = join(qa_t[0], qa_t[1], -qa_t[1], qa_t[0])
    right = jnp.pad(jnp.concatenate(qb_t, 1).astype(BF16), ((pad, pad), (0, 0)))

    levels = len(bits_of(facets))
    slab_shape = (2, SUB, SUB)
    limit = 60 * 1024 * 1024
    slabs = pl.pallas_call(
        functools.partial(transform_kernel, facets),
        out_shape=jax.ShapeDtypeStruct((facets,) + slab_shape, BF16),
        in_specs=[SMEM, VMEM, VMEM, VMEM],
        out_specs=VMEM,
        compiler_params=pltpu.CompilerParams(vmem_limit_bytes=limit),
        name="transform",
    )(targets, facet_spec, left, right)

    grid = pl.pallas_call(
        functools.partial(halve_kernel, facets),
        out_shape=jax.ShapeDtypeStruct(slab_shape, BF16),
        in_specs=[VMEM],
        out_specs=VMEM,
        scratch_shapes=[
            pltpu.VMEM((facets,) + slab_shape, BF16),
            pltpu.VMEM((levels, facets) + slab_shape, BF16),
            pltpu.SemaphoreType.DMA((2 * levels, facets)),
            pltpu.SemaphoreType.DMA((2 * levels, facets)),
        ],
        compiler_params=pltpu.CompilerParams(
            collective_id=0, has_side_effects=True, vmem_limit_bytes=limit
        ),
        name="sum_grids",
    )(slabs)

    residual, gridded = pl.pallas_call(
        vis_kernel,
        out_shape=(
            jax.ShapeDtypeStruct((1, 2, slots), F32),
            jax.ShapeDtypeStruct(slab_shape, BF16),
        ),
        in_specs=[SMEM, VMEM, VMEM, VMEM, VMEM],
        out_specs=(VMEM, VMEM),
        scratch_shapes=[
            pltpu.VMEM((2 * SUB, SUB), BF16),
            pltpu.VMEM((SUB, 2 * SUB), F32),
        ],
        compiler_params=pltpu.CompilerParams(vmem_limit_bytes=limit),
        name="visibilities",
    )(vis_count, grid, bin_offsets, bin_fractions, observed)

    everyone = pl.pallas_call(
        functools.partial(gather_kernel, facets),
        out_shape=jax.ShapeDtypeStruct((facets,) + slab_shape, BF16),
        in_specs=[VMEM],
        out_specs=VMEM,
        scratch_shapes=[
            pltpu.VMEM((facets,) + slab_shape, BF16),
            pltpu.SemaphoreType.DMA((2, facets)),
            pltpu.SemaphoreType.DMA((2, facets)),
        ],
        compiler_params=pltpu.CompilerParams(
            collective_id=1, has_side_effects=True, vmem_limit_bytes=limit
        ),
        name="gather_grids",
    )(gridded)

    chunk = rows // pos_v
    pieces = pl.pallas_call(
        functools.partial(adjoint_kernel, facets),
        out_shape=jax.ShapeDtypeStruct((pos_v, 2, chunk, cols), BF16),
        in_specs=[SMEM, VMEM, VMEM, VMEM],
        out_specs=VMEM,
        scratch_shapes=[pltpu.VMEM((2, rows, cols), F32)],
        compiler_params=pltpu.CompilerParams(vmem_limit_bytes=limit),
        name="adjoint",
    )(targets, everyone, left_adjoint, right)

    update = pl.pallas_call(
        functools.partial(spread_kernel, pos_v),
        out_shape=jax.ShapeDtypeStruct((1, 2, chunk, cols), F32),
        in_specs=[VMEM],
        out_specs=VMEM,
        scratch_shapes=[
            pltpu.VMEM((pos_v - 1, 2, chunk, cols), BF16),
            pltpu.SemaphoreType.DMA((pos_v - 1,)),
            pltpu.SemaphoreType.DMA((pos_v - 1,)),
        ],
        compiler_params=pltpu.CompilerParams(
            collective_id=2, has_side_effects=True, vmem_limit_bytes=limit
        ),
        name="sum_pieces",
    )(pieces)
    return (residual, update)


def solution(mesh):
    placed = (
        P("facet", None, None, None),
        P(),
        P(("facet", "sub")),
        P(("facet", "sub"), None, None),
        P(("facet", "sub"), None, None),
        P(("facet", "sub"), None, None),
    )
    return jax.shard_map(
        on_device,
        mesh=mesh,
        in_specs=placed,
        out_specs=(P(("facet", "sub"), None, None), P("facet", None, "sub", None)),
        check_vma=False,
    )
```

```python
import functools
import math

import jax
import jax.numpy as jnp
import numpy as np
from jax import lax
from jax.experimental import pallas as pl
from jax.experimental.pallas import tpu as pltpu
from jax.sharding import PartitionSpec as P

SUB = 256
MC = 256
STEP = 64
KS = 8
VB = 512
MESH = pl.DeviceIdType.MESH
VMEM = pl.BlockSpec(memory_space=pltpu.VMEM)
SMEM = pl.BlockSpec(memory_space=pltpu.SMEM)
F32 = jnp.float32
BF16 = jnp.bfloat16


def flip(index, bit):
    return index + bit - 2 * bit * ((index // bit) % 2)


def bits_of(count):
    return [1 << level for level in range(count.bit_length() - 1)]


def routes(count):
    bits = bits_of(count)
    return (bits, bits[:1] + bits[:0:-1])


def greet(count):
    me = lax.axis_index("facet")
    barrier = pltpu.get_barrier_semaphore()
    bits = bits_of(count)
    for bit in bits:
        pl.semaphore_signal(
            barrier, inc=1, device_id={"facet": flip(me, bit)}, device_id_type=MESH
        )
    pl.semaphore_wait(barrier, len(bits))


def remote(src, dst, send, recv, axis, target):
    return pltpu.make_async_remote_copy(
        src_ref=src,
        dst_ref=dst,
        send_sem=send,
        recv_sem=recv,
        device_id={axis: target},
        device_id_type=MESH,
    )


def transform_kernel(
    facets, pos_v, base, turns, worker, spec, slabs, left_adjoint, right_table, corners, left_table, holder
):
    cols = spec.shape[3]
    pad = (pos_v - 1) * STEP
    me = lax.axis_index("facet")
    rank = lax.axis_index("sub")

    def note(subgrid, carry):
        holder[worker[subgrid]] = subgrid
        return carry

    lax.fori_loop(0, worker.shape[0], note, 0)
    for slab in range(facets):
        member = me
        for bit in bits_of(facets):
            member = flip(member, bit) if slab & bit else member
        subgrid = holder[member * pos_v + rank]
        corners[0, slab] = subgrid // pos_v * STEP
        corners[1, slab] = pad - subgrid % pos_v * STEP

    def turned(facet):
        turn = turns[facet]
        real, imag = turn[0:1], turn[1:2]
        return (base[0] * real - base[1] * imag, base[0] * imag + base[1] * real)

    real, imag = turned(me)
    left_adjoint[:MC, :SUB] = real.astype(BF16)
    left_adjoint[:MC, SUB:] = imag.astype(BF16)
    left_adjoint[MC:, :SUB] = (-imag).astype(BF16)
    left_adjoint[MC:, SUB:] = real.astype(BF16)
    real, imag = real.T, imag.T
    left_table[:SUB, :MC] = real.astype(BF16)
    left_table[:SUB, MC:] = (-imag).astype(BF16)
    left_table[SUB:, :MC] = imag.astype(BF16)
    left_table[SUB:, MC:] = real.astype(BF16)
    real, imag = turned((5 * me + 3) % facets)
    right_table[:pad] = jnp.zeros((pad, 2 * SUB), BF16)
    right_table[pad + MC :] = jnp.zeros((pad, 2 * SUB), BF16)
    right_table[pad : pad + MC, :SUB] = real.astype(BF16)
    right_table[pad : pad + MC, SUB:] = imag.astype(BF16)

    def transform(slab, carry):
        top = pl.multiple_of(corners[0, slab], STEP)
        left = pl.multiple_of(corners[1, slab], STEP)
        window = jnp.concatenate(
            [spec[0, 0, pl.ds(top, MC), :], spec[0, 1, pl.ds(top, MC), :]], axis=0
        )
        table = right_table[pl.ds(left, cols), :]
        mixed = jnp.dot(window, table, preferred_element_type=F32)
        real = mixed[:MC, :SUB] - mixed[MC:, SUB:]
        imag = mixed[:MC, SUB:] + mixed[MC:, :SUB]
        half = jnp.concatenate([real, imag], axis=0).astype(BF16)
        value = jnp.dot(left_table[...], half, preferred_element_type=F32)
        slabs[slab] = value.astype(BF16).reshape(2, SUB, SUB)
        return carry

    lax.fori_loop(0, facets, transform, 0, unroll=2)


def halve_kernel(facets, slabs, grid_out, total, landed, send, recv):
    me = lax.axis_index("facet")
    greet(facets)
    orders = routes(facets)
    levels = len(orders[0])
    sent = []

    def queue(part, level, held):
        rank = lambda slab: tuple(not slab & bit for bit in orders[part][level:])
        return sorted(held, key=rank)

    def copy_of(source, level, slab, part):
        bit = orders[part][level]
        return remote(
            source.at[slab, part], landed.at[level, slab - bit, part],
            send.at[2 * level + part, slab], recv.at[2 * level + part, slab - bit],
            "facet", flip(me, bit),
        )

    def post(source, level, slab, part):
        copy = copy_of(source, level, slab, part)
        copy.start()
        sent.append(copy)

    held = [list(range(facets))] * 2
    pairs = [queue(part, 0, [s for s in held[part] if s & 1]) for part in range(2)]
    for both in zip(*pairs):
        for part, slab in enumerate(both):
            post(slabs, 0, slab, part)
    for level in range(levels):
        held = [[s for s in held[p] if not s & orders[p][level]] for p in range(2)]
        pairs = [queue(part, level + 1, held[part]) for part in range(2)]
        for both in zip(*pairs):
            for part, slab in enumerate(both):
                copy_of(slabs, level, slab + orders[part][level], part).wait_recv()
                source = slabs if level == 0 else total
                value = source[slab, part].astype(F32) + landed[level, slab, part].astype(F32)
                if level == levels - 1:
                    grid_out[part] = value.astype(BF16)
                else:
                    total[slab, part] = value.astype(BF16)
                    if slab & orders[part][level + 1]:
                        post(total, level + 1, slab, part)
    for copy in sent:
        copy.wait_send()


def kernel_columns(offsets, fractions):
    cells = lax.broadcasted_iota(jnp.int32, (SUB, offsets.shape[1]), 0).astype(F32)
    scale = math.sqrt(math.log2(math.e)) * 9.0 / KS
    centred = cells - (offsets.astype(F32) + (0.5 * KS - 0.5))
    distance = centred * scale - (fractions - 0.5) * scale
    inside = jnp.abs(centred) < 0.5 * KS
    return jnp.where(inside, jnp.exp2(-1.0 - distance * distance), 0.0).astype(BF16)


def vis_kernel(count, grid, offsets, fractions, observed, residual, gridded, flipped, total):
    slots = offsets.shape[2]
    live_count = count[0]
    flipped[:SUB] = grid[0].astype(F32).T.astype(BF16)
    flipped[SUB:] = grid[1].astype(F32).T.astype(BF16)
    total[...] = jnp.zeros_like(total)
    residual[...] = jnp.zeros_like(residual)

    def block(index, carry):
        first = pl.multiple_of(index * VB, VB)
        span = pl.ds(first, VB)
        u_weights = kernel_columns(offsets[0, 0:1, span], fractions[0, 0:1, span])
        v_weights = kernel_columns(offsets[0, 1:2, span], fractions[0, 1:2, span])
        v_float = v_weights.astype(F32)
        product = jnp.dot(flipped[...], u_weights, preferred_element_type=F32)
        live = first + lax.broadcasted_iota(jnp.int32, (1, VB), 1) < live_count
        weighted = []
        for part in range(2):
            model = jnp.sum(product[part * SUB : (part + 1) * SUB] * v_float, axis=0, keepdims=True)
            row = jnp.where(live, observed[0, part : part + 1, span] - model, 0.0)
            residual[0, part : part + 1, span] = row
            weighted.append((row * v_float).astype(BF16))
        total[...] += lax.dot_general(
            u_weights,
            jnp.concatenate(weighted, axis=0),
            (((1,), (1,)), ((), ())),
            preferred_element_type=F32,
        )
        return carry

    lax.fori_loop(0, (live_count + VB - 1) // VB, block, 0)
    gridded[0] = total[:, :SUB].astype(BF16)
    gridded[1] = total[:, SUB:].astype(BF16)


def gather_kernel(facets, own, slabs, send, recv):
    me = lax.axis_index("facet")
    greet(facets)
    orders = [order[:0:-1] + order[:1] for order in routes(facets)]
    levels = len(orders[0])
    sent = []

    def copy_of(level, slab, part):
        bit = orders[part][level]
        source = slabs.at[slab, part] if slab else own.at[part]
        return remote(
            source, slabs.at[slab + bit, part],
            send.at[part, slab + bit], recv.at[part, slab + bit],
            "facet", flip(me, bit),
        )

    def post(level, slab, part):
        copy = copy_of(level, slab, part)
        copy.start()
        sent.append(copy)

    for level in range(levels):
        for part in range(2):
            post(level, 0, part)
    slabs[0] = own[...]
    held = [[0], [0]]
    for level in range(levels):
        for both in zip(*held):
            for part, slab in enumerate(both):
                copy_of(level, slab, part).wait_recv()
                for later in range(level + 1, levels):
                    post(later, slab + orders[part][level], part)
        held = [held[p] + [s + orders[p][level] for s in held[p]] for p in range(2)]
    for copy in sent:
        copy.wait_send()


def adjoint_kernel(facets, targets, everyone, left_table, right_table, pieces, plane):
    cols = plane.shape[2]
    chunk = pieces.shape[2]
    plane[...] = jnp.zeros_like(plane)

    def add_source(slab, carry):
        top = pl.multiple_of(targets[0, slab], STEP)
        left = pl.multiple_of(targets[1, slab], STEP)
        source = everyone[slab].reshape(2 * SUB, SUB)
        half = jnp.dot(left_table[...], source, preferred_element_type=F32)
        real = half[:MC]
        imag = half[MC:]
        stacked = jnp.concatenate(
            [jnp.concatenate([real, imag], axis=1), jnp.concatenate([imag, -real], axis=1)], axis=0
        ).astype(BF16)
        table = right_table[pl.ds(left, cols), :]
        window = lax.dot_general(
            stacked, table, (((1,), (1,)), ((), ())), preferred_element_type=F32
        )
        plane[0, pl.ds(top, MC), :] += window[:MC]
        plane[1, pl.ds(top, MC), :] += window[MC:]
        return carry

    lax.fori_loop(0, facets, add_source, 0, unroll=2)
    for piece in range(pieces.shape[0]):
        pieces[piece] = plane[:, piece * chunk : (piece + 1) * chunk, :].astype(BF16)


def line_kernel(groups, pieces, update, totals, landed, send, recv):
    me = lax.axis_index("sub")
    barrier = pltpu.get_barrier_semaphore()
    inner = (me > 0, me < groups - 1)
    ends = (me == 0, me == groups - 1)
    ahead = ((me + 1) % groups, (me + groups - 1) % groups)
    behind = (ahead[1], ahead[0])
    for way in range(2):
        @pl.when(inner[way])
        def _():
            pl.semaphore_signal(
                barrier, inc=1, device_id={"sub": behind[way]}, device_id_type=MESH
            )
    between = jnp.logical_and(inner[0], inner[1])

    @pl.when(between)
    def _():
        pl.semaphore_wait(barrier, 2)

    @pl.when(jnp.logical_not(between))
    def _():
        pl.semaphore_wait(barrier, 1)

    def copy_of(source, way, chunk, part):
        return remote(
            source, landed.at[way, chunk, part],
            send.at[way, chunk, part], recv.at[way, chunk, part], "sub", ahead[way],
        )

    def sends(way, chunk):
        return me < chunk if way == 0 else me > chunk

    steps = [
        (way, chunk if way == 0 else groups - 1 - chunk, part)
        for chunk in range(groups - 1, 0, -1)
        for part in range(2)
        for way in range(2)
    ]
    for way, chunk, part in steps:
        @pl.when(ends[way])
        def _():
            copy_of(pieces.at[chunk, part], way, chunk, part).start()

        @pl.when(jnp.logical_and(inner[way], sends(way, chunk)))
        def _():
            copy_of(pieces.at[chunk, part], way, chunk, part).wait_recv()
            totals[way, chunk, part] = (
                pieces[chunk, part].astype(F32) + landed[way, chunk, part].astype(F32)
            ).astype(BF16)
            copy_of(totals.at[way, chunk, part], way, chunk, part).start()

    for part in range(2):
        update[0, part] = pieces[me, part].astype(F32)
    for part in range(2):
        for way in range(2):
            @pl.when(inner[way])
            def _():
                copy_of(pieces.at[me, part], way, me, part).wait_recv()
                update[0, part] += landed[way, me, part].astype(F32)
    for way, chunk, part in steps:
        @pl.when(sends(way, chunk))
        def _():
            copy_of(pieces.at[chunk, part], way, chunk, part).wait_send()


def phases(facets):
    modulus = SUB * facets
    centred = np.arange(SUB) - SUB // 2
    base = np.exp(2j * np.pi * (np.outer(centred, centred) * facets % modulus) / modulus)
    turn = np.exp(2j * np.pi * (np.outer(np.arange(facets), centred) % modulus) / modulus)
    pair = lambda z: jnp.asarray(np.stack([z.real, z.imag]).astype(np.float32))
    return pair(base * MC ** (-0.5)), jnp.swapaxes(pair(turn), 0, 1)


def on_device(facet_spec, worker_of_subgrid, vis_count, bin_offsets, bin_fractions, observed):
    facets = lax.axis_size("facet")
    pos_v = lax.axis_size("sub")
    rows = facet_spec.shape[2]
    cols = facet_spec.shape[3]
    pad = (pos_v - 1) * STEP
    slots = bin_offsets.shape[2]
    base, turns = phases(facets)
    levels = len(bits_of(facets))
    slab_shape = (2, SUB, SUB)
    limit = 60 * 1024 * 1024
    slabs, left_adjoint, right, corners = pl.pallas_call(
        functools.partial(transform_kernel, facets, pos_v),
        out_shape=(
            jax.ShapeDtypeStruct((facets,) + slab_shape, BF16),
            jax.ShapeDtypeStruct((2 * MC, 2 * SUB), BF16),
            jax.ShapeDtypeStruct((MC + 2 * pad, 2 * SUB), BF16),
            jax.ShapeDtypeStruct((2, facets), jnp.int32),
        ),
        in_specs=[VMEM, VMEM, SMEM, VMEM],
        out_specs=(VMEM, VMEM, VMEM, SMEM),
        scratch_shapes=[
            pltpu.VMEM((2 * SUB, 2 * MC), BF16),
            pltpu.SMEM(worker_of_subgrid.shape, jnp.int32),
        ],
        compiler_params=pltpu.CompilerParams(vmem_limit_bytes=limit),
        name="transform",
    )(base, turns, worker_of_subgrid, facet_spec)

    grid = pl.pallas_call(
        functools.partial(halve_kernel, facets),
        out_shape=jax.ShapeDtypeStruct(slab_shape, BF16),
        in_specs=[VMEM],
        out_specs=VMEM,
        scratch_shapes=[
            pltpu.VMEM((facets,) + slab_shape, BF16),
            pltpu.VMEM((levels, facets) + slab_shape, BF16),
            pltpu.SemaphoreType.DMA((2 * levels, facets)),
            pltpu.SemaphoreType.DMA((2 * levels, facets)),
        ],
        compiler_params=pltpu.CompilerParams(
            collective_id=0, has_side_effects=True, vmem_limit_bytes=limit
        ),
        name="sum_grids",
    )(slabs)

    residual, gridded = pl.pallas_call(
        vis_kernel,
        out_shape=(
            jax.ShapeDtypeStruct((1, 2, slots), F32),
            jax.ShapeDtypeStruct(slab_shape, BF16),
        ),
        in_specs=[SMEM, VMEM, VMEM, VMEM, VMEM],
        out_specs=(VMEM, VMEM),
        scratch_shapes=[
            pltpu.VMEM((2 * SUB, SUB), BF16),
            pltpu.VMEM((SUB, 2 * SUB), F32),
        ],
        compiler_params=pltpu.CompilerParams(vmem_limit_bytes=limit),
        name="visibilities",
    )(vis_count, grid, bin_offsets, bin_fractions, observed)

    everyone = pl.pallas_call(
        functools.partial(gather_kernel, facets),
        out_shape=jax.ShapeDtypeStruct((facets,) + slab_shape, BF16),
        in_specs=[VMEM],
        out_specs=VMEM,
        scratch_shapes=[
            pltpu.SemaphoreType.DMA((2, facets)),
            pltpu.SemaphoreType.DMA((2, facets)),
        ],
        compiler_params=pltpu.CompilerParams(
            collective_id=1, has_side_effects=True, vmem_limit_bytes=limit
        ),
        name="gather_grids",
    )(gridded)

    chunk = rows // pos_v
    pieces = pl.pallas_call(
        functools.partial(adjoint_kernel, facets),
        out_shape=jax.ShapeDtypeStruct((pos_v, 2, chunk, cols), BF16),
        in_specs=[SMEM, VMEM, VMEM, VMEM],
        out_specs=VMEM,
        scratch_shapes=[pltpu.VMEM((2, rows, cols), F32)],
        compiler_params=pltpu.CompilerParams(vmem_limit_bytes=limit),
        name="adjoint",
    )(corners, everyone, left_adjoint, right)

    update = pl.pallas_call(
        functools.partial(line_kernel, pos_v),
        out_shape=jax.ShapeDtypeStruct((1, 2, chunk, cols), F32),
        in_specs=[VMEM],
        out_specs=VMEM,
        scratch_shapes=[
            pltpu.VMEM((2, pos_v, 2, chunk, cols), BF16),
            pltpu.VMEM((2, pos_v, 2, chunk, cols), BF16),
            pltpu.SemaphoreType.DMA((2, pos_v, 2)),
            pltpu.SemaphoreType.DMA((2, pos_v, 2)),
        ],
        compiler_params=pltpu.CompilerParams(
            collective_id=2, has_side_effects=True, vmem_limit_bytes=limit
        ),
        name="sum_pieces",
    )(pieces)
    return (residual, update)


def solution(mesh):
    placed = (
        P("facet", None, None, None),
        P(),
        P(("facet", "sub")),
        P(("facet", "sub"), None, None),
        P(("facet", "sub"), None, None),
        P(("facet", "sub"), None, None),
    )
    return jax.shard_map(
        on_device,
        mesh=mesh,
        in_specs=placed,
        out_specs=(P(("facet", "sub"), None, None), P("facet", None, "sub", None)),
        check_vma=False,
    )
```

```python
import functools
import math

import jax
import jax.numpy as jnp
import numpy as np
from jax import lax
from jax.experimental import pallas as pl
from jax.experimental.pallas import tpu as pltpu
from jax.sharding import PartitionSpec as P

SUB = 256
MC = 256
STEP = 64
KS = 8
VB = 512
MESH = pl.DeviceIdType.MESH
VMEM = pl.BlockSpec(memory_space=pltpu.VMEM)
SMEM = pl.BlockSpec(memory_space=pltpu.SMEM)
F32 = jnp.float32
BF16 = jnp.bfloat16


def flip(index, bit):
    return index + bit - 2 * bit * ((index // bit) % 2)


def bits_of(count):
    return [1 << level for level in range(count.bit_length() - 1)]


def routes(count):
    bits = bits_of(count)
    return (bits, bits[:1] + bits[:0:-1])


def greet(count):
    me = lax.axis_index("facet")
    barrier = pltpu.get_barrier_semaphore()
    bits = bits_of(count)
    for bit in bits:
        pl.semaphore_signal(
            barrier, inc=1, device_id={"facet": flip(me, bit)}, device_id_type=MESH
        )
    pl.semaphore_wait(barrier, len(bits))


def remote(src, dst, send, recv, axis, target):
    return pltpu.make_async_remote_copy(
        src_ref=src,
        dst_ref=dst,
        send_sem=send,
        recv_sem=recv,
        device_id={axis: target},
        device_id_type=MESH,
    )


def transform_kernel(
    facets, pos_v, base, turns, worker, spec, slabs, left_adjoint, right_table,
    turned_table, corners, left_table, holder
):
    cols = spec.shape[3]
    pad = (pos_v - 1) * STEP
    me = lax.axis_index("facet")
    rank = lax.axis_index("sub")

    def note(subgrid, carry):
        holder[worker[subgrid]] = subgrid
        return carry

    lax.fori_loop(0, worker.shape[0], note, 0)
    for slab in range(facets):
        member = me
        for bit in bits_of(facets):
            member = flip(member, bit) if slab & bit else member
        subgrid = holder[member * pos_v + rank]
        corners[0, slab] = subgrid // pos_v * STEP
        corners[1, slab] = pad - subgrid % pos_v * STEP

    def turned(facet):
        turn = turns[facet]
        real, imag = turn[0:1], turn[1:2]
        return (base[0] * real - base[1] * imag, base[0] * imag + base[1] * real)

    real, imag = turned(me)
    left_adjoint[:MC, :SUB] = real.astype(BF16)
    left_adjoint[:MC, SUB:] = imag.astype(BF16)
    left_adjoint[MC:, :SUB] = (-imag).astype(BF16)
    left_adjoint[MC:, SUB:] = real.astype(BF16)
    real, imag = real.T, imag.T
    left_table[:SUB, :MC] = real.astype(BF16)
    left_table[:SUB, MC:] = (-imag).astype(BF16)
    left_table[SUB:, :MC] = imag.astype(BF16)
    left_table[SUB:, MC:] = real.astype(BF16)
    real, imag = turned((5 * me + 3) % facets)
    for table, first, second in ((right_table, real, imag), (turned_table, -imag, real)):
        table[:pad] = jnp.zeros((pad, 2 * SUB), BF16)
        table[pad + MC :] = jnp.zeros((pad, 2 * SUB), BF16)
        table[pad : pad + MC, :SUB] = first.astype(BF16)
        table[pad : pad + MC, SUB:] = second.astype(BF16)

    def transform(slab, carry):
        top = pl.multiple_of(corners[0, slab], STEP)
        left = pl.multiple_of(corners[1, slab], STEP)
        window = jnp.concatenate(
            [spec[0, 0, pl.ds(top, MC), :], spec[0, 1, pl.ds(top, MC), :]], axis=0
        )
        table = right_table[pl.ds(left, cols), :]
        mixed = jnp.dot(window, table, preferred_element_type=F32)
        real = mixed[:MC, :SUB] - mixed[MC:, SUB:]
        imag = mixed[:MC, SUB:] + mixed[MC:, :SUB]
        half = jnp.concatenate([real, imag], axis=0).astype(BF16)
        value = jnp.dot(left_table[...], half, preferred_element_type=F32)
        slabs[slab] = value.astype(BF16).reshape(2, SUB, SUB)
        return carry

    lax.fori_loop(0, facets, transform, 0, unroll=2)


def halve_kernel(facets, slabs, grid_out, total, landed, send, recv):
    me = lax.axis_index("facet")
    greet(facets)
    orders = routes(facets)
    levels = len(orders[0])
    sent = []

    def queue(part, level, held):
        rank = lambda slab: tuple(not slab & bit for bit in orders[part][level:])
        return sorted(held, key=rank)

    def copy_of(source, level, slab, part):
        bit = orders[part][level]
        return remote(
            source.at[slab, part], landed.at[level, slab - bit, part],
            send.at[2 * level + part, slab], recv.at[2 * level + part, slab - bit],
            "facet", flip(me, bit),
        )

    def post(source, level, slab, part):
        copy = copy_of(source, level, slab, part)
        copy.start()
        sent.append(copy)

    held = [list(range(facets))] * 2
    pairs = [queue(part, 0, [s for s in held[part] if s & 1]) for part in range(2)]
    for both in zip(*pairs):
        for part, slab in enumerate(both):
            post(slabs, 0, slab, part)
    for level in range(levels):
        held = [[s for s in held[p] if not s & orders[p][level]] for p in range(2)]
        pairs = [queue(part, level + 1, held[part]) for part in range(2)]
        for both in zip(*pairs):
            for part, slab in enumerate(both):
                copy_of(slabs, level, slab + orders[part][level], part).wait_recv()
                source = slabs if level == 0 else total
                value = source[slab, part].astype(F32) + landed[level, slab, part].astype(F32)
                if level == levels - 1:
                    grid_out[part] = value.astype(BF16)
                else:
                    total[slab, part] = value.astype(BF16)
                    if slab & orders[part][level + 1]:
                        post(total, level + 1, slab, part)
    for copy in sent:
        copy.wait_send()


def kernel_columns(offsets, fractions):
    cells = lax.broadcasted_iota(jnp.int32, (SUB, offsets.shape[1]), 0).astype(F32)
    scale = math.sqrt(math.log2(math.e)) * 9.0 / KS
    centred = cells - (offsets.astype(F32) + (0.5 * KS - 0.5))
    distance = centred * scale - (fractions - 0.5) * scale
    inside = jnp.abs(centred) < 0.5 * KS
    return jnp.where(inside, jnp.exp2(-1.0 - distance * distance), 0.0).astype(BF16)


def vis_kernel(count, grid, offsets, fractions, observed, residual, gridded, flipped, total):
    slots = offsets.shape[2]
    live_count = count[0]
    flipped[:SUB] = grid[0].astype(F32).T.astype(BF16)
    flipped[SUB:] = grid[1].astype(F32).T.astype(BF16)
    total[...] = jnp.zeros_like(total)
    residual[...] = jnp.zeros_like(residual)

    def half_block(first):
        span = pl.ds(first, VB)
        u_weights = kernel_columns(offsets[0, 0:1, span], fractions[0, 0:1, span])
        v_weights = kernel_columns(offsets[0, 1:2, span], fractions[0, 1:2, span])
        v_float = v_weights.astype(F32)
        product = jnp.dot(flipped[...], u_weights, preferred_element_type=F32)
        live = first + lax.broadcasted_iota(jnp.int32, (1, VB), 1) < live_count
        weighted = []
        for part in range(2):
            model = jnp.sum(product[part * SUB : (part + 1) * SUB] * v_float, axis=0, keepdims=True)
            row = jnp.where(live, observed[0, part : part + 1, span] - model, 0.0)
            residual[0, part : part + 1, span] = row
            weighted.append((row * v_float).astype(BF16))
        return lax.dot_general(
            u_weights,
            jnp.concatenate(weighted, axis=0),
            (((1,), (1,)), ((), ())),
            preferred_element_type=F32,
        )

    def block(index, carry):
        first = pl.multiple_of(index * 2 * VB, 2 * VB)
        total[...] += half_block(first) + half_block(first + VB)
        return carry

    lax.fori_loop(0, (live_count + 2 * VB - 1) // (2 * VB), block, 0)
    gridded[0] = total[:, :SUB].astype(BF16)
    gridded[1] = total[:, SUB:].astype(BF16)


def gather_kernel(facets, own, slabs, send, recv):
    me = lax.axis_index("facet")
    greet(facets)
    orders = [order[:0:-1] + order[:1] for order in routes(facets)]
    levels = len(orders[0])
    sent = []

    def copy_of(level, slab, part):
        bit = orders[part][level]
        source = slabs.at[slab, part] if slab else own.at[part]
        return remote(
            source, slabs.at[slab + bit, part],
            send.at[part, slab + bit], recv.at[part, slab + bit],
            "facet", flip(me, bit),
        )

    def post(level, slab, part):
        copy = copy_of(level, slab, part)
        copy.start()
        sent.append(copy)

    for level in range(levels):
        for part in range(2):
            post(level, 0, part)
    slabs[0] = own[...]
    held = [[0], [0]]
    for level in range(levels):
        for both in zip(*held):
            for part, slab in enumerate(both):
                copy_of(level, slab, part).wait_recv()
                for later in range(level + 1, levels):
                    post(later, slab + orders[part][level], part)
        held = [held[p] + [s + orders[p][level] for s in held[p]] for p in range(2)]
    for copy in sent:
        copy.wait_send()


def adjoint_kernel(facets, corners, everyone, left_table, right_table, turned_table, pieces, plane):
    cols = plane.shape[1] // 2
    chunk = pieces.shape[1]
    plane[...] = jnp.zeros_like(plane)

    def add_source(slab, carry):
        top = pl.multiple_of(corners[0, slab], STEP)
        left = pl.multiple_of(corners[1, slab], STEP)
        source = everyone[slab].reshape(2 * SUB, SUB)
        half = jnp.dot(left_table[...], source, preferred_element_type=F32)
        row = jnp.concatenate([half[:MC], half[MC:]], axis=1).astype(BF16)
        table = jnp.concatenate(
            [right_table[pl.ds(left, cols), :], turned_table[pl.ds(left, cols), :]], axis=0
        )
        window = lax.dot_general(row, table, (((1,), (1,)), ((), ())), preferred_element_type=F32)
        plane[pl.ds(top, MC), :] += window
        return carry

    lax.fori_loop(0, facets, add_source, 0, unroll=2)
    for piece in range(pieces.shape[0]):
        pieces[piece] = plane[piece * chunk : (piece + 1) * chunk, :].astype(BF16)


def line_kernel(groups, pieces, update, totals, landed, send, recv):
    me = lax.axis_index("sub")
    barrier = pltpu.get_barrier_semaphore()
    inner = (me > 0, me < groups - 1)
    ahead = ((me + 1) % groups, (me + groups - 1) % groups)
    behind = (ahead[1], ahead[0])
    for way in range(2):
        @pl.when(inner[way])
        def _():
            pl.semaphore_signal(
                barrier, inc=1, device_id={"sub": behind[way]}, device_id_type=MESH
            )
    between = jnp.logical_and(inner[0], inner[1])

    @pl.when(between)
    def _():
        pl.semaphore_wait(barrier, 2)

    @pl.when(jnp.logical_not(between))
    def _():
        pl.semaphore_wait(barrier, 1)

    cols = update.shape[3]
    size = pieces.shape[1]
    cut = (size // 2 + 15) // 16 * 16
    spans = (pl.ds(0, cut), pl.ds(cut, size - cut))

    def copy_of(source, way, chunk, part):
        return remote(
            source.at[chunk, spans[part]], landed.at[way, chunk, spans[part]],
            send.at[way, chunk, part], recv.at[way, chunk, part], "sub", ahead[way],
        )

    def plan(place):
        steps = []
        for way in range(2):
            depth = place if way == 0 else groups - 1 - place
            for turn in range(2 * (groups - 1 - depth)):
                chunk = turn // 2 if way else groups - 1 - turn // 2
                steps.append((turn + depth, depth, way, chunk, turn % 2))
        return sorted(steps)

    for place in range(groups):
        @pl.when(me == place)
        def _():
            for _, depth, way, chunk, part in plan(place):
                if depth == 0:
                    copy_of(pieces, way, chunk, part).start()
                    continue
                copy_of(pieces, way, chunk, part).wait_recv()
                totals[way, chunk, spans[part]] = (
                    pieces[chunk, spans[part]].astype(F32)
                    + landed[way, chunk, spans[part]].astype(F32)
                ).astype(BF16)
                copy_of(totals.at[way], way, chunk, part).start()
            for part in range(2):
                span = spans[part]
                value = pieces[place, span].astype(F32)
                for way in range(2):
                    if place != (0, groups - 1)[way]:
                        copy_of(pieces, way, place, part).wait_recv()
                        value = value + landed[way, place, span].astype(F32)
                update[0, 0, span] = value[:, :cols]
                update[0, 1, span] = value[:, cols:]
            for _, depth, way, chunk, part in plan(place):
                copy_of(pieces, way, chunk, part).wait_send()


def phases(facets):
    modulus = SUB * facets
    centred = np.arange(SUB) - SUB // 2
    base = np.exp(2j * np.pi * (np.outer(centred, centred) * facets % modulus) / modulus)
    turn = np.exp(2j * np.pi * (np.outer(np.arange(facets), centred) % modulus) / modulus)
    pair = lambda z: jnp.asarray(np.stack([z.real, z.imag]).astype(np.float32))
    return pair(base * MC ** (-0.5)), jnp.swapaxes(pair(turn), 0, 1)


def on_device(facet_spec, worker_of_subgrid, vis_count, bin_offsets, bin_fractions, observed):
    facets = lax.axis_size("facet")
    pos_v = lax.axis_size("sub")
    rows = facet_spec.shape[2]
    cols = facet_spec.shape[3]
    pad = (pos_v - 1) * STEP
    slots = bin_offsets.shape[2]
    base, turns = phases(facets)
    levels = len(bits_of(facets))
    slab_shape = (2, SUB, SUB)
    limit = 60 * 1024 * 1024
    slabs, left_adjoint, right, right_turned, corners = pl.pallas_call(
        functools.partial(transform_kernel, facets, pos_v),
        out_shape=(
            jax.ShapeDtypeStruct((facets,) + slab_shape, BF16),
            jax.ShapeDtypeStruct((2 * MC, 2 * SUB), BF16),
            jax.ShapeDtypeStruct((MC + 2 * pad, 2 * SUB), BF16),
            jax.ShapeDtypeStruct((MC + 2 * pad, 2 * SUB), BF16),
            jax.ShapeDtypeStruct((2, facets), jnp.int32),
        ),
        in_specs=[VMEM, VMEM, SMEM, VMEM],
        out_specs=(VMEM, VMEM, VMEM, VMEM, SMEM),
        scratch_shapes=[
            pltpu.VMEM((2 * SUB, 2 * MC), BF16),
            pltpu.SMEM(worker_of_subgrid.shape, jnp.int32),
        ],
        compiler_params=pltpu.CompilerParams(vmem_limit_bytes=limit),
        name="transform",
    )(base, turns, worker_of_subgrid, facet_spec)

    grid = pl.pallas_call(
        functools.partial(halve_kernel, facets),
        out_shape=jax.ShapeDtypeStruct(slab_shape, BF16),
        in_specs=[VMEM],
        out_specs=VMEM,
        scratch_shapes=[
            pltpu.VMEM((facets,) + slab_shape, BF16),
            pltpu.VMEM((levels, facets) + slab_shape, BF16),
            pltpu.SemaphoreType.DMA((2 * levels, facets)),
            pltpu.SemaphoreType.DMA((2 * levels, facets)),
        ],
        compiler_params=pltpu.CompilerParams(
            collective_id=0, has_side_effects=True, vmem_limit_bytes=limit
        ),
        name="sum_grids",
    )(slabs)

    residual, gridded = pl.pallas_call(
        vis_kernel,
        out_shape=(
            jax.ShapeDtypeStruct((1, 2, slots), F32),
            jax.ShapeDtypeStruct(slab_shape, BF16),
        ),
        in_specs=[SMEM, VMEM, VMEM, VMEM, VMEM],
        out_specs=(VMEM, VMEM),
        scratch_shapes=[
            pltpu.VMEM((2 * SUB, SUB), BF16),
            pltpu.VMEM((SUB, 2 * SUB), F32),
        ],
        compiler_params=pltpu.CompilerParams(vmem_limit_bytes=limit),
        name="visibilities",
    )(vis_count, grid, bin_offsets, bin_fractions, observed)

    everyone = pl.pallas_call(
        functools.partial(gather_kernel, facets),
        out_shape=jax.ShapeDtypeStruct((facets,) + slab_shape, BF16),
        in_specs=[VMEM],
        out_specs=VMEM,
        scratch_shapes=[
            pltpu.SemaphoreType.DMA((2, facets)),
            pltpu.SemaphoreType.DMA((2, facets)),
        ],
        compiler_params=pltpu.CompilerParams(
            collective_id=1, has_side_effects=True, vmem_limit_bytes=limit
        ),
        name="gather_grids",
    )(gridded)

    chunk = rows // pos_v
    pieces = pl.pallas_call(
        functools.partial(adjoint_kernel, facets),
        out_shape=jax.ShapeDtypeStruct((pos_v, chunk, 2 * cols), BF16),
        in_specs=[SMEM, VMEM, VMEM, VMEM, VMEM],
        out_specs=VMEM,
        scratch_shapes=[pltpu.VMEM((rows, 2 * cols), F32)],
        compiler_params=pltpu.CompilerParams(vmem_limit_bytes=limit),
        name="adjoint",
    )(corners, everyone, left_adjoint, right, right_turned)

    update = pl.pallas_call(
        functools.partial(line_kernel, pos_v),
        out_shape=jax.ShapeDtypeStruct((1, 2, chunk, cols), F32),
        in_specs=[VMEM],
        out_specs=VMEM,
        scratch_shapes=[
            pltpu.VMEM((2, pos_v, chunk, 2 * cols), BF16),
            pltpu.VMEM((2, pos_v, chunk, 2 * cols), BF16),
            pltpu.SemaphoreType.DMA((2, pos_v, 2)),
            pltpu.SemaphoreType.DMA((2, pos_v, 2)),
        ],
        compiler_params=pltpu.CompilerParams(
            collective_id=2, has_side_effects=True, vmem_limit_bytes=limit
        ),
        name="sum_pieces",
    )(pieces)
    return (residual, update)


def solution(mesh):
    placed = (
        P("facet", None, None, None),
        P(),
        P(("facet", "sub")),
        P(("facet", "sub"), None, None),
        P(("facet", "sub"), None, None),
        P(("facet", "sub"), None, None),
    )
    return jax.shard_map(
        on_device,
        mesh=mesh,
        in_specs=placed,
        out_specs=(P(("facet", "sub"), None, None), P("facet", None, "sub", None)),
        check_vma=False,
    )
```
